32 devices in a mesh: section: 2 (over x), bits: 4 (over z), rep: 4 (over y, core).
Axes of the slice: x: 2, y: 2, z: 4, core: 2. Of those that a mesh axis runs over, the one named last changes fastest.
Arguments:
- left_stems: bfloat16 [8, 1024, 2, 4, 256], P('rep', 'section', None, 'bits'), may hold values from -6 to 6
- right_stems: bfloat16 [8, 1024, 2, 256], P('rep', 'section'), may hold values from -6 to 6
- left_gate: bfloat16 [2, 256, 256], replicated, may hold values from -0.25 to 0.25
- mix_gate: bfloat16 [2, 256, 256], replicated, may hold values from -0.25 to 0.25
- right_gate: bfloat16 [2, 256, 256], replicated, may hold values from -0.25 to 0.25
- left_low: int32 [4096], P('bits'), may hold values from 0 to 255
- right_index: int32 [4096], P('bits'), may hold values from 0 to 255
Outputs:
- amplitudes: float32 [2, 4096], P(None, 'bits')
The draws below stay inside these ranges and needn't reach their ends.
Inputs may be any that keep to these rules, and one draw needn't show every extreme that they name: Bitstring t has left index (t // 1024) * 256 + left_low[t].
All inputs are finite; a program needn't handle non-finite values.
Results may differ from the reference program's by a relative error of at most 0.015.
Values may be sent and summed in bfloat16 or wider, within the bound.
A program may use at most 128 MiB of HBM per device.

```python
import math
import jax
import jax.numpy as jnp
from jax import lax

LO = 256
NT_DEV = 1024
SLICES = 8
BOND = 1024
HI = 4
LB = 64
NT = 4096
N_BITS = 4


def set_ends(entries, stream_key, smallest, largest):
    longest = entries.shape.index(max(entries.shape))
    spots = []
    for shift in (0, 1):
        where = [jax.random.randint(jax.random.fold_in(stream_key, axis), (), 0, length) for axis, length in enumerate(entries.shape)]
        where[longest] = (where[longest] + shift) % entries.shape[longest]
        spots.append(tuple(where))
    return entries.at[spots[0]].set(smallest).at[spots[1]].set(largest)


def level_of(key, dims, split, low, high):
    loudness, own = 1.0, jax.random.fold_in(key, 6)
    for axis_at, shards_of in split:
        heights = jnp.exp(jax.random.uniform(jax.random.fold_in(own, axis_at), (shards_of,), jnp.float32, low / len(split), high / len(split)))
        loudness = loudness * jnp.repeat(heights, dims[axis_at] // shards_of).reshape([-1 if axis == axis_at else 1 for axis in range(len(dims))])
    return loudness


def bell_draw(key, shape, scale, reach, split=(), dtype=jnp.bfloat16):
    values = scale * jax.random.normal(key, shape, jnp.float32)
    if split:
        values = values * level_of(key, shape, split, -0.22, 0.18)
    return jnp.clip(values, -reach, reach).astype(dtype)


def setup_inputs(seed: int = 0) -> dict:
    streams_of = jax.random.split(jax.random.key(seed), 8)
    left_stems = bell_draw(streams_of[0], (SLICES, BOND, 2, HI, LO), 1.0, 6.0, ((0, 4), (1, 2), (3, 4)))
    right_stems = bell_draw(streams_of[1], (SLICES, BOND, 2, LO), 1.0, 6.0, ((0, 4), (1, 2)))
    left_gate = bell_draw(streams_of[2], (2, LO, LO), (2 * LO) ** -0.5, 0.25)
    mix_gate = bell_draw(streams_of[3], (2, LO, LO), (2 * LO) ** -0.5, 0.25)
    right_gate = bell_draw(streams_of[4], (2, LO, LO), (2 * LO) ** -0.5, 0.25)
    left_low = set_ends(jax.random.randint(streams_of[5], (NT,), 0, LO), jax.random.fold_in(streams_of[5], 1), 0, LO - 1).astype(jnp.int32)
    right_index = set_ends(jax.random.randint(streams_of[6], (NT,), 0, LO), jax.random.fold_in(streams_of[6], 1), 0, LO - 1).astype(jnp.int32)
    return dict(left_stems=left_stems, right_stems=right_stems, left_gate=left_gate, mix_gate=mix_gate, right_gate=right_gate, left_low=left_low, right_index=right_index)


def complex_matrix(gate):
    real_part = gate[0]
    imag_part = gate[1]
    upper_half = jnp.concatenate([real_part, imag_part], axis=1)
    bottom = jnp.concatenate([-imag_part, real_part], axis=1)
    return jnp.concatenate([upper_half, bottom], axis=0)

def reference(left_stems, right_stems, left_gate, mix_gate, right_gate, left_low, right_index):
    first_matrix = complex_matrix(left_gate)
    second_matrix = complex_matrix(mix_gate)
    right_matrix = complex_matrix(right_gate)

    def one_slice(totals, pair):
        left_slice, right_slice = pair
        stem_rows = jnp.transpose(left_slice, (0, 2, 1, 3)).reshape(BOND * HI, 2 * LO)
        first_pass = jnp.dot(stem_rows, first_matrix, preferred_element_type=jnp.float32).astype(jnp.bfloat16)
        first_pass = first_pass.reshape(BOND, HI, 2, N_BITS, LB)
        regrouped = jnp.transpose(first_pass, (3, 0, 2, 1, 4)).reshape(N_BITS * BOND, 2 * LO)
        left_final = jnp.dot(regrouped, second_matrix, preferred_element_type=jnp.float32).astype(jnp.bfloat16)
        left_final = left_final.reshape(N_BITS, BOND, 2, LO)
        right_final = jnp.dot(right_slice.reshape(BOND, 2 * LO), right_matrix, preferred_element_type=jnp.float32).astype(jnp.bfloat16)
        right_final = right_final.reshape(BOND, 2, LO)
        products = jnp.einsum('jkcm,kdn->jcdmn', left_final.astype(jnp.float32), right_final.astype(jnp.float32))
        table_real = products[:, 0, 0] - products[:, 1, 1]
        table_imag = products[:, 0, 1] + products[:, 1, 0]
        return (totals + jnp.stack([table_real, table_imag]), None)
    empty = jnp.zeros((2, N_BITS, LO, LO), jnp.float32)
    table, _ = lax.scan(one_slice, empty, (left_stems, right_stems))
    owner_block = (jnp.arange(NT) // NT_DEV).astype(jnp.int32)
    norm_factor = 1.0 / math.sqrt(SLICES * BOND)
    picked = table[:, owner_block, left_low, right_index]
    return picked * norm_factor
```

```python
import functools
import math

import jax
import jax.numpy as jnp
from jax import lax
from jax.experimental import pallas as pl
from jax.experimental.pallas import tpu as pltpu
from jax.sharding import PartitionSpec as P

MESH = pl.DeviceIdType.MESH
CHUNKS = 4


def flip(index, mask, size):
    total, place = 0, 1
    while place < size:
        bit = lax.rem(index // place, 2)
        total = total + (1 - bit if (mask // place) % 2 else bit) * place
        place *= 2
    return total


def dot(a, b):
    return jnp.dot(a, b, preferred_element_type=jnp.float32)


def dot_t(a, b):
    return lax.dot_general(a, b, (((0,), (0,)), ((), ())), preferred_element_type=jnp.float32)


def onehot(index_rows, width):
    lanes = index_rows.shape[1]
    spots = lax.broadcasted_iota(jnp.int32, (width, lanes), 0)
    parts = [
        jnp.where(spots == index_rows[s : s + 1, :], 1.0, 0.0).astype(jnp.bfloat16)
        for s in range(index_rows.shape[0])
    ]
    return jnp.concatenate(parts, axis=1)


def kernel(
    sizes, norm,
    left_hbm, right_hbm, left_gate_hbm, mix_hbm, right_gate_hbm, low_ref, right_index_ref,
    out_ref,
    left_buf, right_buf, left_gate, mix_rows, right_gate, u_ref,
    idx_buf, z_send, z_recv, plane,
    load_sem, gate_sem, idx_send_sem, idx_recv_sem, z_send_sem, z_recv_sem, p_send_sem, p_recv_sem,
):
    groups, sections, reps = sizes
    me, sec, rep = lax.axis_index("bits"), lax.axis_index("section"), lax.axis_index("rep")
    width = left_gate.shape[1]
    low_width = width // groups
    z_peers = [(x, {"bits": flip(me, x, groups)}) for x in range(1, groups)]
    plane_peers = []
    for a in range(sections):
        for b in range(reps):
            if a or b:
                s, r = flip(sec, a, sections), flip(rep, b, reps)
                plane_peers.append((s * reps + r, {"section": s, "rep": r}, a * reps + b))

    barrier = pltpu.get_barrier_semaphore()
    for _, peer in z_peers:
        pl.semaphore_signal(barrier, inc=1, device_id=peer, device_id_type=MESH)
    for _, peer, _ in plane_peers:
        pl.semaphore_signal(barrier, inc=1, device_id=peer, device_id_type=MESH)

    rows = left_buf.shape[0]
    step = rows // CHUNKS
    left_rows, right_rows = left_hbm.reshape(rows, width), right_hbm.reshape(rows, width)
    loads = []
    for c in range(CHUNKS):
        at = pl.ds(c * step, step)
        pair = (
            pltpu.make_async_copy(right_rows.at[at], right_buf.at[at], load_sem.at[0, c]),
            pltpu.make_async_copy(left_rows.at[at], left_buf.at[at], load_sem.at[1, c]),
        )
        for copy in pair:
            copy.start()
        loads.append(pair)
    mine = pl.ds(pl.multiple_of(me * low_width, low_width), low_width)
    gate_loads = [
        pltpu.make_async_copy(left_gate_hbm, left_gate, gate_sem.at[0]),
        pltpu.make_async_copy(right_gate_hbm, right_gate, gate_sem.at[1]),
        pltpu.make_async_copy(mix_hbm.at[:, mine, :], mix_rows, gate_sem.at[2]),
    ]
    for copy in gate_loads:
        copy.start()

    block = min(width, step)
    row_at = lax.broadcasted_iota(jnp.int32, (block, block), 0)
    column_at = lax.broadcasted_iota(jnp.int32, (block, block), 1)
    swap = jnp.where(row_at + 1 - 2 * lax.rem(row_at, 2) == column_at, 1.0, 0.0).astype(jnp.bfloat16)
    parity = lax.rem(lax.broadcasted_iota(jnp.int32, (block, width), 0), 2)
    sign = (1 - 2 * parity).astype(jnp.float32).astype(jnp.bfloat16)
    total = jnp.zeros((width, 2 * width), jnp.float32)
    for c in range(CHUNKS):
        for copy in loads[c]:
            copy.wait()
        pieces = []
        for b in range(step // block):
            at = pl.ds(c * step + b * block, block)
            r = right_buf[at, :]
            pieces.append(jnp.concatenate([r * sign, dot(swap, r).astype(jnp.bfloat16)], axis=1))
        total = total + dot_t(left_buf[pl.ds(c * step, step), :], jnp.concatenate(pieces, axis=0))
    q = total.astype(jnp.bfloat16)

    pl.semaphore_wait(barrier, len(z_peers) + len(plane_peers))
    idx_copies = []
    for x, peer in z_peers:
        for w, ref in enumerate((low_ref, right_index_ref)):
            copy = pltpu.make_async_remote_copy(
                src_ref=ref, dst_ref=idx_buf.at[x, w],
                send_sem=idx_send_sem.at[x, w], recv_sem=idx_recv_sem.at[x, w],
                device_id=peer, device_id_type=MESH,
            )
            copy.start()
            idx_copies.append(copy)

    for copy in gate_loads:
        copy.wait()
    g0, g1 = dot_t(left_gate[0], q), dot_t(left_gate[1], q)
    t_real = (g0[:, :width] - g1[:, width:]).astype(jnp.bfloat16)
    t_imag = (g0[:, width:] + g1[:, :width]).astype(jnp.bfloat16)
    t = jnp.concatenate([t_real, t_imag], axis=0)
    h0, h1 = dot(t, right_gate[0]), dot(t, right_gate[1])
    u_ref[0] = h0[:width] - h1[width:]
    u_ref[1] = h0[width:] + h1[:width]
    mix = jnp.concatenate([mix_rows[0], mix_rows[1]], axis=0)

    def amplitudes(j, low, right, write):
        at = pl.ds(pl.multiple_of(j * low_width, low_width), low_width)
        u = jnp.concatenate([u_ref[0, at, :], u_ref[1, at, :]], axis=0).astype(jnp.bfloat16)
        index_rows, lanes = low.shape
        part = 2 if index_rows % 2 == 0 else 1
        for k in range(0, index_rows, part):
            x = dot(mix, onehot(low[k : k + part], width))
            v = dot(u, onehot(right[k : k + part], width))
            x0, x1, v0, v1 = x[:low_width], x[low_width:], v[:low_width], v[low_width:]
            real = jnp.sum(x0 * v0 - x1 * v1, axis=0, keepdims=True)
            imag = jnp.sum(x0 * v1 + x1 * v0, axis=0, keepdims=True)
            write(pl.ds(k * lanes, part * lanes), real, imag)

    def write_to(ref, slot):
        def write(at, real, imag):
            ref[slot, 0:1, at] = real
            ref[slot, 1:2, at] = imag

        return write

    amplitudes(me, low_ref[...], right_index_ref[...], write_to(z_recv, 0))

    z_copies = []
    for n, (x, peer) in enumerate(z_peers):
        idx_copies[2 * n].wait_recv()
        idx_copies[2 * n + 1].wait_recv()
        amplitudes(peer["bits"], idx_buf[x, 0], idx_buf[x, 1], write_to(z_send, x))
        copy = pltpu.make_async_remote_copy(
            src_ref=z_send.at[x], dst_ref=z_recv.at[x],
            send_sem=z_send_sem.at[x], recv_sem=z_recv_sem.at[x],
            device_id=peer, device_id_type=MESH,
        )
        copy.start()
        z_copies.append(copy)

    own = z_recv[0]
    for x in range(1, groups):
        z_copies[x - 1].wait_recv()
        own = own + z_recv[x]
    here = sec * reps + rep
    plane[here] = own
    p_copies = []
    for there, peer, n in plane_peers:
        copy = pltpu.make_async_remote_copy(
            src_ref=plane.at[here], dst_ref=plane.at[here],
            send_sem=p_send_sem.at[n], recv_sem=p_recv_sem.at[n],
            device_id=peer, device_id_type=MESH,
        )
        copy.start()
        p_copies.append(copy)
    for copy in p_copies:
        copy.wait_recv()
    result = plane[0]
    for n in range(1, sections * reps):
        result = result + plane[n]
    out_ref[...] = result * norm
    for copy in idx_copies + z_copies + p_copies:
        copy.wait_send()


def body(left_stems, right_stems, left_gate, mix_gate, right_gate, left_low, right_index):
    width = left_gate.shape[1]
    sizes = tuple(lax.axis_size(name) for name in ("bits", "section", "rep"))
    groups, sections, reps = sizes
    pairs = left_stems.shape[0] * left_stems.shape[1]
    norm = 1.0 / math.sqrt(pairs * sections * reps)
    count = left_low.shape[0]
    index_shape = (count // 128, 128)
    bf16, f32 = jnp.bfloat16, jnp.float32
    hbm = pl.BlockSpec(memory_space=pltpu.HBM)
    vmem = pl.BlockSpec(memory_space=pltpu.VMEM)
    dma = pltpu.SemaphoreType.DMA
    return pl.pallas_call(
        functools.partial(kernel, sizes, norm),
        out_shape=jax.ShapeDtypeStruct((2, count), f32),
        in_specs=[hbm] * 5 + [vmem] * 2,
        out_specs=vmem,
        scratch_shapes=[
            pltpu.VMEM((2 * pairs, width), bf16),
            pltpu.VMEM((2 * pairs, width), bf16),
            pltpu.VMEM((2, width, width), bf16),
            pltpu.VMEM((2, width // groups, width), bf16),
            pltpu.VMEM((2, width, width), bf16),
            pltpu.VMEM((2, width, width), f32),
            pltpu.VMEM((groups, 2) + index_shape, jnp.int32),
            pltpu.VMEM((groups, 2, count), f32),
            pltpu.VMEM((groups, 2, count), f32),
            pltpu.VMEM((sections * reps, 2, count), f32),
            dma((2, CHUNKS)),
            dma((3,)),
            dma((groups, 2)),
            dma((groups, 2)),
            dma((groups,)),
            dma((groups,)),
            dma((sections * reps,)),
            dma((sections * reps,)),
        ],
        compiler_params=pltpu.CompilerParams(collective_id=0, has_side_effects=True),
        name="amplitudes",
    )(
        left_stems.reshape(pairs, 2, width), right_stems.reshape(pairs, 2, width),
        left_gate, mix_gate, right_gate,
        left_low.reshape(index_shape), right_index.reshape(index_shape),
    )


def solution(mesh):
    in_specs = (
        P("rep", "section", None, "bits", None),
        P("rep", "section", None, None),
        P(),
        P(),
        P(),
        P("bits"),
        P("bits"),
    )
    out_specs = P(None, "bits")
    return jax.shard_map(body, mesh=mesh, in_specs=in_specs, out_specs=out_specs, check_vma=False)
```

```python
import functools
import math

import jax
import jax.numpy as jnp
from jax import lax
from jax.experimental import pallas as pl
from jax.experimental.pallas import tpu as pltpu
from jax.sharding import PartitionSpec as P

MESH = pl.DeviceIdType.MESH
CHUNKS = 4


def flip(index, mask, size):
    total, place = 0, 1
    while place < size:
        bit = lax.rem(index // place, 2)
        total = total + (1 - bit if (mask // place) % 2 else bit) * place
        place *= 2
    return total


def dot(a, b):
    return jnp.dot(a, b, preferred_element_type=jnp.float32)


def dot_t(a, b):
    return lax.dot_general(a, b, (((0,), (0,)), ((), ())), preferred_element_type=jnp.float32)


def onehot(index_rows, width):
    lanes = index_rows.shape[1]
    spots = lax.broadcasted_iota(jnp.int32, (width, lanes), 0)
    parts = [
        jnp.where(spots == index_rows[s : s + 1, :], 1.0, 0.0).astype(jnp.bfloat16)
        for s in range(index_rows.shape[0])
    ]
    return jnp.concatenate(parts, axis=1)


def kernel(
    sizes, norm,
    left_hbm, right_hbm, left_gate_hbm, mix_hbm, right_gate_hbm, low_hbm, right_index_hbm,
    out_ref,
    left_buf, right_buf, left_gate, mix_rows, right_gate, u_ref,
    idx_buf, own_ref, z_send, z_recv, plane,
    load_sem, gate_sem, idx_send_sem, idx_recv_sem, z_send_sem, z_recv_sem, p_send_sem, p_recv_sem,
):
    groups, sections, reps = sizes
    me, sec, rep = lax.axis_index("bits"), lax.axis_index("section"), lax.axis_index("rep")
    width = left_gate.shape[1]
    low_width = width // groups
    z_peers = [(x, {"bits": flip(me, x, groups)}) for x in range(1, groups)]
    plane_peers = []
    for a in reversed(range(sections)):
        for b in reversed(range(reps)):
            if a or b:
                s, r = flip(sec, a, sections), flip(rep, b, reps)
                plane_peers.append((s * reps + r, {"section": s, "rep": r}, a * reps + b))

    barrier = pltpu.get_barrier_semaphore()
    for _, peer in z_peers:
        pl.semaphore_signal(barrier, inc=1, device_id=peer, device_id_type=MESH)
    for _, peer, _ in plane_peers:
        pl.semaphore_signal(barrier, inc=1, device_id=peer, device_id_type=MESH)

    rows = left_buf.shape[0]
    step = rows // CHUNKS
    left_rows, right_rows = left_hbm.reshape(rows, width), right_hbm.reshape(rows, width)
    loads = []
    for c in range(CHUNKS):
        at = pl.ds(c * step, step)
        pair = (
            pltpu.make_async_copy(right_rows.at[at], right_buf.at[at], load_sem.at[0, c]),
            pltpu.make_async_copy(left_rows.at[at], left_buf.at[at], load_sem.at[1, c]),
        )
        for copy in pair:
            copy.start()
        loads.append(pair)
    mine = pl.ds(pl.multiple_of(me * low_width, low_width), low_width)
    gate_loads = [
        pltpu.make_async_copy(left_gate_hbm, left_gate, gate_sem.at[0]),
        pltpu.make_async_copy(right_gate_hbm, right_gate, gate_sem.at[1]),
        pltpu.make_async_copy(mix_hbm.at[:, mine, :], mix_rows, gate_sem.at[2]),
    ]
    idx_loads = [
        pltpu.make_async_copy(low_hbm, idx_buf.at[0, 0], idx_recv_sem.at[0, 0]),
        pltpu.make_async_copy(right_index_hbm, idx_buf.at[0, 1], idx_recv_sem.at[0, 1]),
    ]
    for copy in idx_loads + gate_loads:
        copy.start()

    block = min(width, step)
    row_at = lax.broadcasted_iota(jnp.int32, (block, block), 0)
    column_at = lax.broadcasted_iota(jnp.int32, (block, block), 1)
    swap = jnp.where(row_at + 1 - 2 * lax.rem(row_at, 2) == column_at, 1.0, 0.0).astype(jnp.bfloat16)
    parity = lax.rem(lax.broadcasted_iota(jnp.int32, (block, width), 0), 2)
    sign = (1 - 2 * parity).astype(jnp.float32).astype(jnp.bfloat16)
    total = jnp.zeros((width, 2 * width), jnp.float32)
    for c in range(CHUNKS):
        for copy in loads[c]:
            copy.wait()
        pieces = []
        for b in range(step // block):
            at = pl.ds(c * step + b * block, block)
            r = right_buf[at, :]
            pieces.append(jnp.concatenate([r * sign, dot(swap, r).astype(jnp.bfloat16)], axis=1))
        total = total + dot_t(left_buf[pl.ds(c * step, step), :], jnp.concatenate(pieces, axis=0))
    q = total.astype(jnp.bfloat16)

    for copy in idx_loads:
        copy.wait()
    pl.semaphore_wait(barrier, len(z_peers) + len(plane_peers))
    idx_copies = []
    for x, peer in z_peers:
        for w in range(2):
            copy = pltpu.make_async_remote_copy(
                src_ref=idx_buf.at[0, w], dst_ref=idx_buf.at[x, w],
                send_sem=idx_send_sem.at[x, w], recv_sem=idx_recv_sem.at[x, w],
                device_id=peer, device_id_type=MESH,
            )
            copy.start()
            idx_copies.append(copy)

    for copy in gate_loads:
        copy.wait()
    g0, g1 = dot_t(left_gate[0], q), dot_t(left_gate[1], q)
    t_real = (g0[:, :width] - g1[:, width:]).astype(jnp.bfloat16)
    t_imag = (g0[:, width:] + g1[:, :width]).astype(jnp.bfloat16)
    t = jnp.concatenate([t_real, t_imag], axis=0)
    h0, h1 = dot(t, right_gate[0]), dot(t, right_gate[1])
    u_ref[0] = h0[:width] - h1[width:]
    u_ref[1] = h0[width:] + h1[:width]
    mix = jnp.concatenate([mix_rows[0], mix_rows[1]], axis=0)

    def amplitudes(j, low, right, write):
        at = pl.ds(pl.multiple_of(j * low_width, low_width), low_width)
        u = jnp.concatenate([u_ref[0, at, :], u_ref[1, at, :]], axis=0).astype(jnp.bfloat16)
        index_rows, lanes = low.shape
        part = 2 if index_rows % 2 == 0 else 1
        for k in range(0, index_rows, part):
            x = dot(mix, onehot(low[k : k + part], width))
            v = dot(u, onehot(right[k : k + part], width))
            x0, x1, v0, v1 = x[:low_width], x[low_width:], v[:low_width], v[low_width:]
            real = jnp.sum(x0 * v0 - x1 * v1, axis=0, keepdims=True)
            imag = jnp.sum(x0 * v1 + x1 * v0, axis=0, keepdims=True)
            write(pl.ds(k * lanes, part * lanes), jnp.concatenate([real, imag], axis=0))

    def write_own(at, value):
        own_ref[:, at] = value

    amplitudes(me, idx_buf[0, 0], idx_buf[0, 1], write_own)

    z_copies = []
    for n, (x, peer) in enumerate(z_peers):
        idx_copies[2 * n].wait_recv()
        idx_copies[2 * n + 1].wait_recv()

        def write_send(at, value, x=x):
            z_send[x, :, at] = value.astype(z_send.dtype)

        amplitudes(peer["bits"], idx_buf[x, 0], idx_buf[x, 1], write_send)
        copy = pltpu.make_async_remote_copy(
            src_ref=z_send.at[x], dst_ref=z_recv.at[x],
            send_sem=z_send_sem.at[x], recv_sem=z_recv_sem.at[x],
            device_id=peer, device_id_type=MESH,
        )
        copy.start()
        z_copies.append(copy)

    own = own_ref[...]
    for x in range(1, groups):
        z_copies[x - 1].wait_recv()
        own = own + z_recv[x].astype(jnp.float32)
    here = sec * reps + rep
    plane[here] = own.astype(plane.dtype)
    p_copies = []
    for there, peer, n in plane_peers:
        copy = pltpu.make_async_remote_copy(
            src_ref=plane.at[here], dst_ref=plane.at[here],
            send_sem=p_send_sem.at[n], recv_sem=p_recv_sem.at[n],
            device_id=peer, device_id_type=MESH,
        )
        copy.start()
        p_copies.append(copy)
    for copy in p_copies:
        copy.wait_recv()
    result = plane[0].astype(jnp.float32)
    for n in range(1, sections * reps):
        result = result + plane[n].astype(jnp.float32)
    out_ref[...] = result * norm
    for copy in idx_copies + z_copies + p_copies:
        copy.wait_send()


def body(left_stems, right_stems, left_gate, mix_gate, right_gate, left_low, right_index):
    width = left_gate.shape[1]
    sizes = tuple(lax.axis_size(name) for name in ("bits", "section", "rep"))
    groups, sections, reps = sizes
    pairs = left_stems.shape[0] * left_stems.shape[1]
    norm = 1.0 / math.sqrt(pairs * sections * reps)
    count = left_low.shape[0]
    index_shape = (count // 128, 128)
    bf16, f32 = jnp.bfloat16, jnp.float32
    hbm = pl.BlockSpec(memory_space=pltpu.HBM)
    vmem = pl.BlockSpec(memory_space=pltpu.VMEM)
    dma = pltpu.SemaphoreType.DMA
    keep = functools.partial(pltpu.with_memory_space_constraint, memory_space=pltpu.HBM)
    return pl.pallas_call(
        functools.partial(kernel, sizes, norm),
        out_shape=jax.ShapeDtypeStruct((2, count), f32),
        in_specs=[hbm] * 7,
        out_specs=vmem,
        scratch_shapes=[
            pltpu.VMEM((2 * pairs, width), bf16),
            pltpu.VMEM((2 * pairs, width), bf16),
            pltpu.VMEM((2, width, width), bf16),
            pltpu.VMEM((2, width // groups, width), bf16),
            pltpu.VMEM((2, width, width), bf16),
            pltpu.VMEM((2, width, width), f32),
            pltpu.VMEM((groups, 2) + index_shape, jnp.int32),
            pltpu.VMEM((2, count), f32),
            pltpu.VMEM((groups, 2, count), bf16),
            pltpu.VMEM((groups, 2, count), bf16),
            pltpu.VMEM((sections * reps, 2, count), bf16),
            dma((2, CHUNKS)),
            dma((3,)),
            dma((groups, 2)),
            dma((groups, 2)),
            dma((groups,)),
            dma((groups,)),
            dma((sections * reps,)),
            dma((sections * reps,)),
        ],
        compiler_params=pltpu.CompilerParams(
            collective_id=0, has_side_effects=True, vmem_limit_bytes=16 * 1024 * 1024
        ),
        name="amplitudes",
    )(
        keep(left_stems.reshape(pairs, 2, width)), keep(right_stems.reshape(pairs, 2, width)),
        keep(left_gate), keep(mix_gate), keep(right_gate),
        keep(left_low.reshape(index_shape)), keep(right_index.reshape(index_shape)),
    )


def solution(mesh):
    in_specs = (
        P("rep", "section", None, "bits", None),
        P("rep", "section", None, None),
        P(),
        P(),
        P(),
        P("bits"),
        P("bits"),
    )
    out_specs = P(None, "bits")
    return jax.shard_map(body, mesh=mesh, in_specs=in_specs, out_specs=out_specs, check_vma=False)
```

```python
import functools
import math

import jax
import jax.numpy as jnp
from jax import lax
from jax.experimental import pallas as pl
from jax.experimental.pallas import tpu as pltpu
from jax.sharding import PartitionSpec as P

MESH = pl.DeviceIdType.MESH
CHUNKS = 4


def flip(index, mask, size):
    total, place = 0, 1
    while place < size:
        bit = lax.rem(index // place, 2)
        total = total + (1 - bit if (mask // place) % 2 else bit) * place
        place *= 2
    return total


def dot(a, b):
    return jnp.dot(a, b, preferred_element_type=jnp.float32)


def dot_t(a, b):
    return lax.dot_general(a, b, (((0,), (0,)), ((), ())), preferred_element_type=jnp.float32)


def onehot(index_rows, width):
    lanes = index_rows.shape[1]
    spots = lax.broadcasted_iota(jnp.int32, (width, lanes), 0)
    parts = [
        jnp.where(spots == index_rows[s : s + 1, :], 1.0, 0.0).astype(jnp.bfloat16)
        for s in range(index_rows.shape[0])
    ]
    return jnp.concatenate(parts, axis=1)


def kernel(
    sizes, norm,
    left_hbm, right_hbm, left_gate_hbm, mix_hbm, right_gate_hbm, low_hbm, right_index_hbm,
    out_ref,
    left_buf, right_buf, left_gate, mix_rows, right_gate, u_ref, mix_far, u_send, u_recv,
    idx_buf, own_ref, z_send, z_recv, plane,
    load_sem, gate_sem, idx_send_sem, idx_recv_sem, z_send_sem, z_recv_sem, p_send_sem, p_recv_sem, u_sem,
):
    groups, sections, reps = sizes
    me, sec, rep = lax.axis_index("bits"), lax.axis_index("section"), lax.axis_index("rep")
    width = left_gate.shape[1]
    low_width = width // groups
    last = groups - 1
    z_peers = [(x, {"bits": flip(me, x, groups)}) for x in [1, last] + list(range(2, last)) if x <= last]
    if groups == 2:
        z_peers = z_peers[:1]
    far = jnp.logical_or(me == 0, me == last)
    far_peer = {"bits": flip(me, last, groups)}
    far_rows = pl.ds(pl.multiple_of(far_peer["bits"] * low_width, low_width), low_width)

    def unless_far(x, run):
        if x == last:
            pl.when(jnp.logical_not(far))(run)
        else:
            run()

    plane_peers = []
    for a in reversed(range(sections)):
        for b in reversed(range(reps)):
            if a or b:
                s, r = flip(sec, a, sections), flip(rep, b, reps)
                plane_peers.append((s * reps + r, {"section": s, "rep": r}, a * reps + b))

    barrier = pltpu.get_barrier_semaphore()
    for _, peer in z_peers:
        pl.semaphore_signal(barrier, inc=1, device_id=peer, device_id_type=MESH)
    for _, peer, _ in plane_peers:
        pl.semaphore_signal(barrier, inc=1, device_id=peer, device_id_type=MESH)

    rows = left_buf.shape[0]
    step = rows // CHUNKS
    left_rows, right_rows = left_hbm.reshape(rows, width), right_hbm.reshape(rows, width)
    loads = []
    for c in range(CHUNKS):
        at = pl.ds(c * step, step)
        pair = (
            pltpu.make_async_copy(right_rows.at[at], right_buf.at[at], load_sem.at[0, c]),
            pltpu.make_async_copy(left_rows.at[at], left_buf.at[at], load_sem.at[1, c]),
        )
        for copy in pair:
            copy.start()
        loads.append(pair)
    mine = pl.ds(pl.multiple_of(me * low_width, low_width), low_width)
    gate_loads = [
        pltpu.make_async_copy(left_gate_hbm, left_gate, gate_sem.at[0]),
        pltpu.make_async_copy(right_gate_hbm, right_gate, gate_sem.at[1]),
        pltpu.make_async_copy(mix_hbm.at[:, mine, :], mix_rows, gate_sem.at[2]),
        pltpu.make_async_copy(mix_hbm.at[:, far_rows, :], mix_far, gate_sem.at[3]),
    ]
    idx_loads = [
        pltpu.make_async_copy(low_hbm, idx_buf.at[0, 0], idx_recv_sem.at[0, 0]),
        pltpu.make_async_copy(right_index_hbm, idx_buf.at[0, 1], idx_recv_sem.at[0, 1]),
    ]
    for copy in idx_loads + gate_loads:
        copy.start()

    block = min(width, step)
    row_at = lax.broadcasted_iota(jnp.int32, (block, block), 0)
    column_at = lax.broadcasted_iota(jnp.int32, (block, block), 1)
    swap = jnp.where(row_at + 1 - 2 * lax.rem(row_at, 2) == column_at, 1.0, 0.0).astype(jnp.bfloat16)
    parity = lax.rem(lax.broadcasted_iota(jnp.int32, (block, width), 0), 2)
    sign = (1 - 2 * parity).astype(jnp.float32).astype(jnp.bfloat16)
    total = jnp.zeros((width, 2 * width), jnp.float32)
    for c in range(CHUNKS):
        for copy in loads[c]:
            copy.wait()
        pieces = []
        for b in range(step // block):
            at = pl.ds(c * step + b * block, block)
            r = right_buf[at, :]
            pieces.append(jnp.concatenate([r * sign, dot(swap, r).astype(jnp.bfloat16)], axis=1))
        total = total + dot_t(left_buf[pl.ds(c * step, step), :], jnp.concatenate(pieces, axis=0))
    q = total.astype(jnp.bfloat16)

    for copy in idx_loads:
        copy.wait()
    pl.semaphore_wait(barrier, len(z_peers) + len(plane_peers))

    def idx_copies(x, peer):
        return [
            pltpu.make_async_remote_copy(
                src_ref=idx_buf.at[0, w], dst_ref=idx_buf.at[x, w],
                send_sem=idx_send_sem.at[x, w], recv_sem=idx_recv_sem.at[x, w],
                device_id=peer, device_id_type=MESH,
            )
            for w in range(2)
        ]

    def z_copy(x, peer):
        return pltpu.make_async_remote_copy(
            src_ref=z_send.at[x], dst_ref=z_recv.at[x],
            send_sem=z_send_sem.at[x], recv_sem=z_recv_sem.at[x],
            device_id=peer, device_id_type=MESH,
        )

    def u_copy():
        return pltpu.make_async_remote_copy(
            src_ref=u_send, dst_ref=u_recv, send_sem=u_sem.at[0], recv_sem=u_sem.at[1],
            device_id=far_peer, device_id_type=MESH,
        )

    for x, peer in z_peers:

        def send_indices(x=x, peer=peer):
            for copy in idx_copies(x, peer):
                copy.start()

        unless_far(x, send_indices)

    for copy in gate_loads:
        copy.wait()
    g0, g1 = dot_t(left_gate[0], q), dot_t(left_gate[1], q)
    t_real = (g0[:, :width] - g1[:, width:]).astype(jnp.bfloat16)
    t_imag = (g0[:, width:] + g1[:, :width]).astype(jnp.bfloat16)
    t = jnp.concatenate([t_real, t_imag], axis=0)
    h0, h1 = dot(t, right_gate[0]), dot(t, right_gate[1])
    u_ref[0] = h0[:width] - h1[width:]
    u_ref[1] = h0[width:] + h1[:width]

    @pl.when(far)
    def _():
        u_send[...] = u_ref[:, far_rows, :].astype(u_send.dtype)
        u_copy().start()

    def amplitudes(mix_of, u, slot, write):
        mix = jnp.concatenate([mix_of[0], mix_of[1]], axis=0)
        index_rows, lanes = idx_buf.shape[2:]
        part = 2 if index_rows % 2 == 0 else 1
        for k in range(0, index_rows, part):
            x = dot(mix, onehot(idx_buf[slot, 0, k : k + part], width))
            v = dot(u, onehot(idx_buf[slot, 1, k : k + part], width))
            x0, x1, v0, v1 = x[:low_width], x[low_width:], v[:low_width], v[low_width:]
            real = jnp.sum(x0 * v0 - x1 * v1, axis=0, keepdims=True)
            imag = jnp.sum(x0 * v1 + x1 * v0, axis=0, keepdims=True)
            write(pl.ds(k * lanes, part * lanes), jnp.concatenate([real, imag], axis=0))

    def u_of(j):
        at = pl.ds(pl.multiple_of(j * low_width, low_width), low_width)
        return jnp.concatenate([u_ref[0, at, :], u_ref[1, at, :]], axis=0).astype(jnp.bfloat16)

    def write_own(at, value):
        own_ref[:, at] = value

    def add_own(at, value):
        own_ref[:, at] += value

    amplitudes(mix_rows, u_of(me), 0, write_own)

    for x, peer in z_peers:

        def send_partial(x=x, peer=peer):
            def write_send(at, value):
                z_send[x, :, at] = value.astype(z_send.dtype)

            for copy in idx_copies(x, peer):
                copy.wait_recv()
            amplitudes(mix_rows, u_of(peer["bits"]), x, write_send)
            z_copy(x, peer).start()

        unless_far(x, send_partial)

    @pl.when(far)
    def _():
        u_copy().wait_recv()
        u = jnp.concatenate([u_recv[0], u_recv[1]], axis=0)
        amplitudes(mix_far, u, 0, add_own)

    for x, peer in z_peers:

        def add_partial(x=x, peer=peer):
            z_copy(x, peer).wait_recv()
            own_ref[...] += z_recv[x].astype(jnp.float32)

        unless_far(x, add_partial)
    own = own_ref[...]
    here = sec * reps + rep
    plane[here] = own.astype(plane.dtype)
    p_copies = []
    for there, peer, n in plane_peers:
        copy = pltpu.make_async_remote_copy(
            src_ref=plane.at[here], dst_ref=plane.at[here],
            send_sem=p_send_sem.at[n], recv_sem=p_recv_sem.at[n],
            device_id=peer, device_id_type=MESH,
        )
        copy.start()
        p_copies.append(copy)
    for copy in p_copies:
        copy.wait_recv()
    result = plane[0].astype(jnp.float32)
    for n in range(1, sections * reps):
        result = result + plane[n].astype(jnp.float32)
    out_ref[...] = result * norm
    for x, peer in z_peers:

        def finish(x=x, peer=peer):
            for copy in idx_copies(x, peer) + [z_copy(x, peer)]:
                copy.wait_send()

        unless_far(x, finish)

    @pl.when(far)
    def _():
        u_copy().wait_send()

    for copy in p_copies:
        copy.wait_send()


def body(left_stems, right_stems, left_gate, mix_gate, right_gate, left_low, right_index):
    width = left_gate.shape[1]
    sizes = tuple(lax.axis_size(name) for name in ("bits", "section", "rep"))
    groups, sections, reps = sizes
    pairs = left_stems.shape[0] * left_stems.shape[1]
    norm = 1.0 / math.sqrt(pairs * sections * reps)
    count = left_low.shape[0]
    index_shape = (count // 128, 128)
    bf16, f32 = jnp.bfloat16, jnp.float32
    hbm = pl.BlockSpec(memory_space=pltpu.HBM)
    vmem = pl.BlockSpec(memory_space=pltpu.VMEM)
    dma = pltpu.SemaphoreType.DMA
    keep = functools.partial(pltpu.with_memory_space_constraint, memory_space=pltpu.HBM)
    return pl.pallas_call(
        functools.partial(kernel, sizes, norm),
        out_shape=jax.ShapeDtypeStruct((2, count), f32),
        in_specs=[hbm] * 7,
        out_specs=vmem,
        scratch_shapes=[
            pltpu.VMEM((2 * pairs, width), bf16),
            pltpu.VMEM((2 * pairs, width), bf16),
            pltpu.VMEM((2, width, width), bf16),
            pltpu.VMEM((2, width // groups, width), bf16),
            pltpu.VMEM((2, width, width), bf16),
            pltpu.VMEM((2, width, width), f32),
            pltpu.VMEM((2, width // groups, width), bf16),
            pltpu.VMEM((2, width // groups, width), bf16),
            pltpu.VMEM((2, width // groups, width), bf16),
            pltpu.VMEM((groups, 2) + index_shape, jnp.int32),
            pltpu.VMEM((2, count), f32),
            pltpu.VMEM((groups, 2, count), bf16),
            pltpu.VMEM((groups, 2, count), bf16),
            pltpu.VMEM((sections * reps, 2, count), bf16),
            dma((2, CHUNKS)),
            dma((4,)),
            dma((groups, 2)),
            dma((groups, 2)),
            dma((groups,)),
            dma((groups,)),
            dma((sections * reps,)),
            dma((sections * reps,)),
            dma((2,)),
        ],
        compiler_params=pltpu.CompilerParams(
            collective_id=0, has_side_effects=True, vmem_limit_bytes=16 * 1024 * 1024
        ),
        name="amplitudes",
    )(
        keep(left_stems.reshape(pairs, 2, width)), keep(right_stems.reshape(pairs, 2, width)),
        keep(left_gate), keep(mix_gate), keep(right_gate),
        keep(left_low.reshape(index_shape)), keep(right_index.reshape(index_shape)),
    )


def solution(mesh):
    in_specs = (
        P("rep", "section", None, "bits", None),
        P("rep", "section", None, None),
        P(),
        P(),
        P(),
        P("bits"),
        P("bits"),
    )
    out_specs = P(None, "bits")
    return jax.shard_map(body, mesh=mesh, in_specs=in_specs, out_specs=out_specs, check_vma=False)
```

```python
import functools
import math

import jax
import jax.numpy as jnp
from jax import lax
from jax.experimental import pallas as pl
from jax.experimental.pallas import tpu as pltpu
from jax.sharding import PartitionSpec as P

MESH = pl.DeviceIdType.MESH
CHUNKS = 4


def flip(index, mask, size):
    total, place = 0, 1
    while place < size:
        bit = lax.rem(index // place, 2)
        total = total + (1 - bit if (mask // place) % 2 else bit) * place
        place *= 2
    return total


def dot(a, b):
    return jnp.dot(a, b, preferred_element_type=jnp.float32)


def dot_t(a, b):
    return lax.dot_general(a, b, (((0,), (0,)), ((), ())), preferred_element_type=jnp.float32)


def onehot(index_rows, width):
    lanes = index_rows.shape[1]
    spots = lax.broadcasted_iota(jnp.int32, (width, lanes), 0)
    parts = [
        jnp.where(spots == index_rows[s : s + 1, :], 1.0, 0.0).astype(jnp.bfloat16)
        for s in range(index_rows.shape[0])
    ]
    return jnp.concatenate(parts, axis=1)


def kernel(
    sizes, norm,
    left_hbm, right_hbm, left_gate_hbm, mix_hbm, right_gate_hbm, low_hbm, right_index_hbm,
    out_ref,
    left_buf, right_buf, left_gate, mix_rows, right_gate, u_ref,
    idx_buf, own_ref, z_send, z_recv, pair_buf, plane,
    load_sem, gate_sem, idx_send_sem, idx_recv_sem, z_send_sem, z_recv_sem, p_send_sem, p_recv_sem, pair_sem,
):
    groups, sections, reps = sizes
    me, sec, rep = lax.axis_index("bits"), lax.axis_index("section"), lax.axis_index("rep")
    width = left_gate.shape[1]
    low_width = width // groups
    z_peers = [(x, {"bits": flip(me, x, groups)}) for x in range(1, groups)]
    halves = reps // 2
    pair_peer = {"rep": flip(rep, 1, reps)}
    plane_peers = []
    for a in reversed(range(sections)):
        for b in reversed(range(halves)):
            if a or b:
                there = {"section": flip(sec, a, sections), "rep": flip(rep, 2 * b, reps)}
                plane_peers.append((there, a * halves + b))

    barrier = pltpu.get_barrier_semaphore()
    for _, peer in z_peers:
        pl.semaphore_signal(barrier, inc=1, device_id=peer, device_id_type=MESH)
    for peer in [pair_peer] + [peer for peer, _ in plane_peers]:
        pl.semaphore_signal(barrier, inc=1, device_id=peer, device_id_type=MESH)

    rows = left_buf.shape[0]
    step = rows // CHUNKS
    left_rows, right_rows = left_hbm.reshape(rows, width), right_hbm.reshape(rows, width)
    loads = []
    for c in range(CHUNKS):
        at = pl.ds(c * step, step)
        pair = (
            pltpu.make_async_copy(right_rows.at[at], right_buf.at[at], load_sem.at[0, c]),
            pltpu.make_async_copy(left_rows.at[at], left_buf.at[at], load_sem.at[1, c]),
        )
        for copy in pair:
            copy.start()
        loads.append(pair)
    mine = pl.ds(pl.multiple_of(me * low_width, low_width), low_width)
    gate_loads = [
        pltpu.make_async_copy(left_gate_hbm, left_gate, gate_sem.at[0]),
        pltpu.make_async_copy(right_gate_hbm, right_gate, gate_sem.at[1]),
        pltpu.make_async_copy(mix_hbm.at[:, mine, :], mix_rows, gate_sem.at[2]),
    ]
    idx_loads = [
        pltpu.make_async_copy(low_hbm, idx_buf.at[0, 0], idx_recv_sem.at[0, 0]),
        pltpu.make_async_copy(right_index_hbm, idx_buf.at[0, 1], idx_recv_sem.at[0, 1]),
    ]
    for copy in idx_loads + gate_loads:
        copy.start()

    block = min(width, step)
    row_at = lax.broadcasted_iota(jnp.int32, (block, block), 0)
    column_at = lax.broadcasted_iota(jnp.int32, (block, block), 1)
    swap = jnp.where(row_at + 1 - 2 * lax.rem(row_at, 2) == column_at, 1.0, 0.0).astype(jnp.bfloat16)
    parity = lax.rem(lax.broadcasted_iota(jnp.int32, (block, width), 0), 2)
    sign = (1 - 2 * parity).astype(jnp.float32).astype(jnp.bfloat16)
    total = jnp.zeros((width, 2 * width), jnp.float32)
    for c in range(CHUNKS):
        for copy in loads[c]:
            copy.wait()
        pieces = []
        for b in range(step // block):
            at = pl.ds(c * step + b * block, block)
            r = right_buf[at, :]
            pieces.append(jnp.concatenate([r * sign, dot(swap, r).astype(jnp.bfloat16)], axis=1))
        total = total + dot_t(left_buf[pl.ds(c * step, step), :], jnp.concatenate(pieces, axis=0))
    q = total.astype(jnp.bfloat16)

    for copy in idx_loads:
        copy.wait()
    pl.semaphore_wait(barrier, len(z_peers) + 1 + len(plane_peers))
    idx_copies = []
    for x, peer in z_peers:
        for w in range(2):
            copy = pltpu.make_async_remote_copy(
                src_ref=idx_buf.at[0, w], dst_ref=idx_buf.at[x, w],
                send_sem=idx_send_sem.at[x, w], recv_sem=idx_recv_sem.at[x, w],
                device_id=peer, device_id_type=MESH,
            )
            copy.start()
            idx_copies.append(copy)

    for copy in gate_loads:
        copy.wait()
    g0, g1 = dot_t(left_gate[0], q), dot_t(left_gate[1], q)
    t_real = (g0[:, :width] - g1[:, width:]).astype(jnp.bfloat16)
    t_imag = (g0[:, width:] + g1[:, :width]).astype(jnp.bfloat16)
    t = jnp.concatenate([t_real, t_imag], axis=0)
    h0, h1 = dot(t, right_gate[0]), dot(t, right_gate[1])
    u_ref[0] = h0[:width] - h1[width:]
    u_ref[1] = h0[width:] + h1[:width]
    mix = jnp.concatenate([mix_rows[0], mix_rows[1]], axis=0)

    def amplitudes(j, low, right, write):
        at = pl.ds(pl.multiple_of(j * low_width, low_width), low_width)
        u = jnp.concatenate([u_ref[0, at, :], u_ref[1, at, :]], axis=0).astype(jnp.bfloat16)
        index_rows, lanes = low.shape
        part = 2 if index_rows % 2 == 0 else 1
        for k in range(0, index_rows, part):
            x = dot(mix, onehot(low[k : k + part], width))
            v = dot(u, onehot(right[k : k + part], width))
            x0, x1, v0, v1 = x[:low_width], x[low_width:], v[:low_width], v[low_width:]
            real = jnp.sum(x0 * v0 - x1 * v1, axis=0, keepdims=True)
            imag = jnp.sum(x0 * v1 + x1 * v0, axis=0, keepdims=True)
            write(pl.ds(k * lanes, part * lanes), jnp.concatenate([real, imag], axis=0))

    def write_own(at, value):
        own_ref[:, at] = value

    amplitudes(me, idx_buf[0, 0], idx_buf[0, 1], write_own)

    z_copies = []
    for n, (x, peer) in enumerate(z_peers):
        idx_copies[2 * n].wait_recv()
        idx_copies[2 * n + 1].wait_recv()

        def write_send(at, value, x=x):
            z_send[x, :, at] = value.astype(z_send.dtype)

        amplitudes(peer["bits"], idx_buf[x, 0], idx_buf[x, 1], write_send)
        copy = pltpu.make_async_remote_copy(
            src_ref=z_send.at[x], dst_ref=z_recv.at[x],
            send_sem=z_send_sem.at[x], recv_sem=z_recv_sem.at[x],
            device_id=peer, device_id_type=MESH,
        )
        copy.start()
        z_copies.append(copy)

    own = own_ref[...]
    for x in range(1, groups):
        z_copies[x - 1].wait_recv()
        own = own + z_recv[x].astype(jnp.float32)
    side = lax.rem(rep, 2)
    pair_buf[side] = own.astype(pair_buf.dtype)
    pair_copy = pltpu.make_async_remote_copy(
        src_ref=pair_buf.at[side], dst_ref=pair_buf.at[side],
        send_sem=pair_sem.at[0], recv_sem=pair_sem.at[1],
        device_id=pair_peer, device_id_type=MESH,
    )
    pair_copy.start()
    pair_copy.wait_recv()
    here = sec * halves + rep // 2
    plane[here] = (pair_buf[0].astype(jnp.float32) + pair_buf[1].astype(jnp.float32)).astype(plane.dtype)
    p_copies = []
    for peer, n in plane_peers:
        copy = pltpu.make_async_remote_copy(
            src_ref=plane.at[here], dst_ref=plane.at[here],
            send_sem=p_send_sem.at[n], recv_sem=p_recv_sem.at[n],
            device_id=peer, device_id_type=MESH,
        )
        copy.start()
        p_copies.append(copy)
    for copy in p_copies:
        copy.wait_recv()
    result = plane[0].astype(jnp.float32)
    for n in range(1, sections * halves):
        result = result + plane[n].astype(jnp.float32)
    out_ref[...] = result * norm
    for copy in idx_copies + z_copies + [pair_copy] + p_copies:
        copy.wait_send()


def body(left_stems, right_stems, left_gate, mix_gate, right_gate, left_low, right_index):
    width = left_gate.shape[1]
    sizes = tuple(lax.axis_size(name) for name in ("bits", "section", "rep"))
    groups, sections, reps = sizes
    pairs = left_stems.shape[0] * left_stems.shape[1]
    norm = 1.0 / math.sqrt(pairs * sections * reps)
    count = left_low.shape[0]
    index_shape = (count // 128, 128)
    bf16, f32 = jnp.bfloat16, jnp.float32
    hbm = pl.BlockSpec(memory_space=pltpu.HBM)
    vmem = pl.BlockSpec(memory_space=pltpu.VMEM)
    dma = pltpu.SemaphoreType.DMA
    keep = functools.partial(pltpu.with_memory_space_constraint, memory_space=pltpu.HBM)
    return pl.pallas_call(
        functools.partial(kernel, sizes, norm),
        out_shape=jax.ShapeDtypeStruct((2, count), f32),
        in_specs=[hbm] * 7,
        out_specs=vmem,
        scratch_shapes=[
            pltpu.VMEM((2 * pairs, width), bf16),
            pltpu.VMEM((2 * pairs, width), bf16),
            pltpu.VMEM((2, width, width), bf16),
            pltpu.VMEM((2, width // groups, width), bf16),
            pltpu.VMEM((2, width, width), bf16),
            pltpu.VMEM((2, width, width), f32),
            pltpu.VMEM((groups, 2) + index_shape, jnp.int32),
            pltpu.VMEM((2, count), f32),
            pltpu.VMEM((groups, 2, count), bf16),
            pltpu.VMEM((groups, 2, count), bf16),
            pltpu.VMEM((2, 2, count), bf16),
            pltpu.VMEM((sections * reps // 2, 2, count), bf16),
            dma((2, CHUNKS)),
            dma((3,)),
            dma((groups, 2)),
            dma((groups, 2)),
            dma((groups,)),
            dma((groups,)),
            dma((sections * reps // 2,)),
            dma((sections * reps // 2,)),
            dma((2,)),
        ],
        compiler_params=pltpu.CompilerParams(
            collective_id=0, has_side_effects=True, vmem_limit_bytes=16 * 1024 * 1024
        ),
        name="amplitudes",
    )(
        keep(left_stems.reshape(pairs, 2, width)), keep(right_stems.reshape(pairs, 2, width)),
        keep(left_gate), keep(mix_gate), keep(right_gate),
        keep(left_low.reshape(index_shape)), keep(right_index.reshape(index_shape)),
    )


def solution(mesh):
    in_specs = (
        P("rep", "section", None, "bits", None),
        P("rep", "section", None, None),
        P(),
        P(),
        P(),
        P("bits"),
        P("bits"),
    )
    out_specs = P(None, "bits")
    return jax.shard_map(body, mesh=mesh, in_specs=in_specs, out_specs=out_specs, check_vma=False)
```

```python
import functools
import math

import jax
import jax.numpy as jnp
from jax import lax
from jax.experimental import pallas as pl
from jax.experimental.pallas import tpu as pltpu
from jax.sharding import PartitionSpec as P

MESH = pl.DeviceIdType.MESH
CHUNKS = 4


def flip(index, mask, size):
    total, place = 0, 1
    while place < size:
        bit = lax.rem(index // place, 2)
        total = total + (1 - bit if (mask // place) % 2 else bit) * place
        place *= 2
    return total


def dot(a, b):
    return jnp.dot(a, b, preferred_element_type=jnp.float32)


def dot_t(a, b):
    return lax.dot_general(a, b, (((0,), (0,)), ((), ())), preferred_element_type=jnp.float32)


def onehot(index_rows, width):
    lanes = index_rows.shape[1]
    spots = lax.broadcasted_iota(jnp.int32, (width, lanes), 0)
    parts = [
        jnp.where(spots == index_rows[s : s + 1, :], 1.0, 0.0).astype(jnp.bfloat16)
        for s in range(index_rows.shape[0])
    ]
    return jnp.concatenate(parts, axis=1)


def kernel(
    sizes, norm,
    left_hbm, right_hbm, left_gate_hbm, mix_hbm, right_gate_hbm, low_hbm, right_index_hbm,
    out_ref,
    left_buf, right_buf, left_gate, mix_rows, right_gate, u_ref,
    idx_own, idx_buf, own_ref, z_send, z_recv, plane,
    load_sem, gate_sem, idx_send_sem, idx_recv_sem, z_send_sem, z_recv_sem, p_send_sem, p_recv_sem,
):
    groups, sections, reps = sizes
    me, sec, rep = lax.axis_index("bits"), lax.axis_index("section"), lax.axis_index("rep")
    width = left_gate.shape[1]
    low_width = width // groups
    z_peers = [(x, {"bits": flip(me, x, groups)}) for x in range(1, groups)]
    plane_peers = []
    for a in reversed(range(sections)):
        for b in reversed(range(reps)):
            if a or b:
                s, r = flip(sec, a, sections), flip(rep, b, reps)
                plane_peers.append((s * reps + r, {"section": s, "rep": r}, a * reps + b))

    barrier = pltpu.get_barrier_semaphore()
    for _, peer in z_peers:
        pl.semaphore_signal(barrier, inc=1, device_id=peer, device_id_type=MESH)
    for _, peer, _ in plane_peers:
        pl.semaphore_signal(barrier, inc=1, device_id=peer, device_id_type=MESH)

    rows = left_buf.shape[0]
    step = rows // CHUNKS
    left_rows, right_rows = left_hbm.reshape(rows, width), right_hbm.reshape(rows, width)
    loads = []
    for c in range(CHUNKS):
        at = pl.ds(c * step, step)
        pair = (
            pltpu.make_async_copy(right_rows.at[at], right_buf.at[at], load_sem.at[0, c]),
            pltpu.make_async_copy(left_rows.at[at], left_buf.at[at], load_sem.at[1, c]),
        )
        for copy in pair:
            copy.start()
        loads.append(pair)
    mine = pl.ds(pl.multiple_of(me * low_width, low_width), low_width)
    gate_loads = [
        pltpu.make_async_copy(left_gate_hbm, left_gate, gate_sem.at[0]),
        pltpu.make_async_copy(right_gate_hbm, right_gate, gate_sem.at[1]),
        pltpu.make_async_copy(mix_hbm.at[:, mine, :], mix_rows, gate_sem.at[2]),
    ]
    idx_loads = [
        pltpu.make_async_copy(low_hbm, idx_own.at[0], gate_sem.at[3]),
        pltpu.make_async_copy(right_index_hbm, idx_own.at[1], gate_sem.at[4]),
    ]
    for copy in idx_loads + gate_loads:
        copy.start()

    for copy in idx_loads:
        copy.wait()
    idx_buf[0] = idx_own[...].astype(jnp.float32).astype(idx_buf.dtype)

    block = min(width, step)
    row_at = lax.broadcasted_iota(jnp.int32, (block, block), 0)
    column_at = lax.broadcasted_iota(jnp.int32, (block, block), 1)
    swap = jnp.where(row_at + 1 - 2 * lax.rem(row_at, 2) == column_at, 1.0, 0.0).astype(jnp.bfloat16)
    parity = lax.rem(lax.broadcasted_iota(jnp.int32, (block, width), 0), 2)
    sign = (1 - 2 * parity).astype(jnp.float32).astype(jnp.bfloat16)
    total = jnp.zeros((width, 2 * width), jnp.float32)
    for c in range(CHUNKS):
        for copy in loads[c]:
            copy.wait()
        pieces = []
        for b in range(step // block):
            at = pl.ds(c * step + b * block, block)
            r = right_buf[at, :]
            pieces.append(jnp.concatenate([r * sign, dot(swap, r).astype(jnp.bfloat16)], axis=1))
        total = total + dot_t(left_buf[pl.ds(c * step, step), :], jnp.concatenate(pieces, axis=0))
    q = total.astype(jnp.bfloat16)

    pl.semaphore_wait(barrier, len(z_peers) + len(plane_peers))
    idx_copies = []
    for x, peer in z_peers:
        copy = pltpu.make_async_remote_copy(
            src_ref=idx_buf.at[0], dst_ref=idx_buf.at[x],
            send_sem=idx_send_sem.at[x], recv_sem=idx_recv_sem.at[x],
            device_id=peer, device_id_type=MESH,
        )
        copy.start()
        idx_copies.append(copy)

    for copy in gate_loads:
        copy.wait()
    g0, g1 = dot_t(left_gate[0], q), dot_t(left_gate[1], q)
    t_real = (g0[:, :width] - g1[:, width:]).astype(jnp.bfloat16)
    t_imag = (g0[:, width:] + g1[:, :width]).astype(jnp.bfloat16)
    t = jnp.concatenate([t_real, t_imag], axis=0)
    h0, h1 = dot(t, right_gate[0]), dot(t, right_gate[1])
    u_ref[0] = h0[:width] - h1[width:]
    u_ref[1] = h0[width:] + h1[:width]
    mix = jnp.concatenate([mix_rows[0], mix_rows[1]], axis=0)

    def amplitudes(j, low, right, write):
        at = pl.ds(pl.multiple_of(j * low_width, low_width), low_width)
        u = jnp.concatenate([u_ref[0, at, :], u_ref[1, at, :]], axis=0).astype(jnp.bfloat16)
        index_rows, lanes = low.shape
        part = 2 if index_rows % 2 == 0 else 1
        for k in range(0, index_rows, part):
            x = dot(mix, onehot(low[k : k + part], width))
            v = dot(u, onehot(right[k : k + part], width))
            x0, x1, v0, v1 = x[:low_width], x[low_width:], v[:low_width], v[low_width:]
            real = jnp.sum(x0 * v0 - x1 * v1, axis=0, keepdims=True)
            imag = jnp.sum(x0 * v1 + x1 * v0, axis=0, keepdims=True)
            write(pl.ds(k * lanes, part * lanes), jnp.concatenate([real, imag], axis=0))

    def write_own(at, value):
        own_ref[:, at] = value

    amplitudes(me, idx_own[0], idx_own[1], write_own)

    z_copies = []
    for n, (x, peer) in enumerate(z_peers):
        idx_copies[n].wait_recv()
        low, right = idx_buf[x].astype(jnp.float32).astype(jnp.int32)

        def write_send(at, value, x=x):
            z_send[x, :, at] = value.astype(z_send.dtype)

        amplitudes(peer["bits"], low, right, write_send)
        copy = pltpu.make_async_remote_copy(
            src_ref=z_send.at[x], dst_ref=z_recv.at[x],
            send_sem=z_send_sem.at[x], recv_sem=z_recv_sem.at[x],
            device_id=peer, device_id_type=MESH,
        )
        copy.start()
        z_copies.append(copy)

    own = own_ref[...]
    for x in range(1, groups):
        z_copies[x - 1].wait_recv()
        own = own + z_recv[x].astype(jnp.float32)
    here = sec * reps + rep
    plane[here] = own.astype(plane.dtype)
    p_copies = []
    for there, peer, n in plane_peers:
        copy = pltpu.make_async_remote_copy(
            src_ref=plane.at[here], dst_ref=plane.at[here],
            send_sem=p_send_sem.at[n], recv_sem=p_recv_sem.at[n],
            device_id=peer, device_id_type=MESH,
        )
        copy.start()
        p_copies.append(copy)
    for copy in p_copies:
        copy.wait_recv()
    result = plane[0].astype(jnp.float32)
    for n in range(1, sections * reps):
        result = result + plane[n].astype(jnp.float32)
    out_ref[...] = result * norm
    for copy in idx_copies + z_copies + p_copies:
        copy.wait_send()


def body(left_stems, right_stems, left_gate, mix_gate, right_gate, left_low, right_index):
    width = left_gate.shape[1]
    sizes = tuple(lax.axis_size(name) for name in ("bits", "section", "rep"))
    groups, sections, reps = sizes
    pairs = left_stems.shape[0] * left_stems.shape[1]
    norm = 1.0 / math.sqrt(pairs * sections * reps)
    count = left_low.shape[0]
    index_shape = (count // 128, 128)
    bf16, f32 = jnp.bfloat16, jnp.float32
    hbm = pl.BlockSpec(memory_space=pltpu.HBM)
    vmem = pl.BlockSpec(memory_space=pltpu.VMEM)
    dma = pltpu.SemaphoreType.DMA
    keep = functools.partial(pltpu.with_memory_space_constraint, memory_space=pltpu.HBM)
    return pl.pallas_call(
        functools.partial(kernel, sizes, norm),
        out_shape=jax.ShapeDtypeStruct((2, count), f32),
        in_specs=[hbm] * 7,
        out_specs=vmem,
        scratch_shapes=[
            pltpu.VMEM((2 * pairs, width), bf16),
            pltpu.VMEM((2 * pairs, width), bf16),
            pltpu.VMEM((2, width, width), bf16),
            pltpu.VMEM((2, width // groups, width), bf16),
            pltpu.VMEM((2, width, width), bf16),
            pltpu.VMEM((2, width, width), f32),
            pltpu.VMEM((2,) + index_shape, jnp.int32),
            pltpu.VMEM((groups, 2) + index_shape, bf16),
            pltpu.VMEM((2, count), f32),
            pltpu.VMEM((groups, 2, count), bf16),
            pltpu.VMEM((groups, 2, count), bf16),
            pltpu.VMEM((sections * reps, 2, count), bf16),
            dma((2, CHUNKS)),
            dma((5,)),
            dma((groups,)),
            dma((groups,)),
            dma((groups,)),
            dma((groups,)),
            dma((sections * reps,)),
            dma((sections * reps,)),
        ],
        compiler_params=pltpu.CompilerParams(
            collective_id=0, has_side_effects=True, vmem_limit_bytes=16 * 1024 * 1024
        ),
        name="amplitudes",
    )(
        keep(left_stems.reshape(pairs, 2, width)), keep(right_stems.reshape(pairs, 2, width)),
        keep(left_gate), keep(mix_gate), keep(right_gate),
        keep(left_low.reshape(index_shape)), keep(right_index.reshape(index_shape)),
    )


def solution(mesh):
    in_specs = (
        P("rep", "section", None, "bits", None),
        P("rep", "section", None, None),
        P(),
        P(),
        P(),
        P("bits"),
        P("bits"),
    )
    out_specs = P(None, "bits")
    return jax.shard_map(body, mesh=mesh, in_specs=in_specs, out_specs=out_specs, check_vma=False)
```

```python
import functools
import math

import jax
import jax.numpy as jnp
from jax import lax
from jax.experimental import pallas as pl
from jax.experimental.pallas import tpu as pltpu
from jax.sharding import PartitionSpec as P

MESH = pl.DeviceIdType.MESH
CHUNKS = 4


def flip(index, mask, size):
    total, place = 0, 1
    while place < size:
        bit = lax.rem(index // place, 2)
        total = total + (1 - bit if (mask // place) % 2 else bit) * place
        place *= 2
    return total


def dot(a, b):
    return jnp.dot(a, b, preferred_element_type=jnp.float32)


def dot_t(a, b):
    return lax.dot_general(a, b, (((0,), (0,)), ((), ())), preferred_element_type=jnp.float32)


def onehot(index_rows, width):
    lanes = index_rows.shape[1]
    spots = lax.broadcasted_iota(jnp.int32, (width, lanes), 0)
    parts = [
        jnp.where(spots == index_rows[s : s + 1, :], 1.0, 0.0).astype(jnp.bfloat16)
        for s in range(index_rows.shape[0])
    ]
    return jnp.concatenate(parts, axis=1)


def kernel(
    sizes, norm,
    left_hbm, right_hbm, left_gate_hbm, mix_hbm, right_gate_hbm, low_hbm, right_index_hbm,
    out_ref,
    left_buf, right_buf, left_gate, mix_rows, right_gate, u_ref,
    idx_buf, own_ref, z_send, z_recv, plane,
    load_sem, gate_sem, idx_send_sem, idx_recv_sem, z_send_sem, z_recv_sem, p_send_sem, p_recv_sem,
):
    groups, sections, reps = sizes
    me, sec, rep = lax.axis_index("bits"), lax.axis_index("section"), lax.axis_index("rep")
    width = left_gate.shape[1]
    low_width = width // groups
    z_peers = [(x, {"bits": flip(me, x, groups)}) for x in range(1, groups)]
    plane_peers = []
    for a in reversed(range(sections)):
        for b in reversed(range(reps)):
            if a or b:
                s, r = flip(sec, a, sections), flip(rep, b, reps)
                plane_peers.append((s * reps + r, {"section": s, "rep": r}, a * reps + b))

    barrier = pltpu.get_barrier_semaphore()
    for _, peer in z_peers:
        pl.semaphore_signal(barrier, inc=1, device_id=peer, device_id_type=MESH)
    for _, peer, _ in plane_peers:
        pl.semaphore_signal(barrier, inc=1, device_id=peer, device_id_type=MESH)

    rows = left_buf.shape[0]
    step = rows // CHUNKS
    left_rows, right_rows = left_hbm.reshape(rows, width), right_hbm.reshape(rows, width)
    loads = []
    for c in range(CHUNKS):
        at = pl.ds(c * step, step)
        pair = (
            pltpu.make_async_copy(right_rows.at[at], right_buf.at[at], load_sem.at[0, c]),
            pltpu.make_async_copy(left_rows.at[at], left_buf.at[at], load_sem.at[1, c]),
        )
        for copy in pair:
            copy.start()
        loads.append(pair)
    mine = pl.ds(pl.multiple_of(me * low_width, low_width), low_width)
    gate_loads = [
        pltpu.make_async_copy(left_gate_hbm, left_gate, gate_sem.at[0]),
        pltpu.make_async_copy(right_gate_hbm, right_gate, gate_sem.at[1]),
        pltpu.make_async_copy(mix_hbm.at[:, mine, :], mix_rows, gate_sem.at[2]),
    ]
    idx_loads = [
        pltpu.make_async_copy(low_hbm, idx_buf.at[0, 0], idx_recv_sem.at[0, 0]),
        pltpu.make_async_copy(right_index_hbm, idx_buf.at[0, 1], idx_recv_sem.at[0, 1]),
    ]
    for copy in idx_loads + gate_loads:
        copy.start()

    for copy in idx_loads:
        copy.wait()
    pl.semaphore_wait(barrier, len(z_peers) + len(plane_peers))
    idx_copies = []
    for x, peer in z_peers:
        for w in range(2):
            copy = pltpu.make_async_remote_copy(
                src_ref=idx_buf.at[0, w], dst_ref=idx_buf.at[x, w],
                send_sem=idx_send_sem.at[x, w], recv_sem=idx_recv_sem.at[x, w],
                device_id=peer, device_id_type=MESH,
            )
            copy.start()
            idx_copies.append(copy)

    block = min(width, step)
    row_at = lax.broadcasted_iota(jnp.int32, (block, block), 0)
    column_at = lax.broadcasted_iota(jnp.int32, (block, block), 1)
    swap = jnp.where(row_at + 1 - 2 * lax.rem(row_at, 2) == column_at, 1.0, 0.0).astype(jnp.bfloat16)
    parity = lax.rem(lax.broadcasted_iota(jnp.int32, (block, width), 0), 2)
    sign = (1 - 2 * parity).astype(jnp.float32).astype(jnp.bfloat16)
    total = jnp.zeros((width, 2 * width), jnp.float32)
    for c in range(CHUNKS):
        for copy in loads[c]:
            copy.wait()
        pieces = []
        for b in range(step // block):
            at = pl.ds(c * step + b * block, block)
            r = right_buf[at, :]
            pieces.append(jnp.concatenate([r * sign, dot(swap, r).astype(jnp.bfloat16)], axis=1))
        total = total + dot_t(left_buf[pl.ds(c * step, step), :], jnp.concatenate(pieces, axis=0))
    q = total.astype(jnp.bfloat16)

    for copy in gate_loads:
        copy.wait()
    g0, g1 = dot_t(left_gate[0], q), dot_t(left_gate[1], q)
    t_real = (g0[:, :width] - g1[:, width:]).astype(jnp.bfloat16)
    t_imag = (g0[:, width:] + g1[:, :width]).astype(jnp.bfloat16)
    t = jnp.concatenate([t_real, t_imag], axis=0)
    h0, h1 = dot(t, right_gate[0]), dot(t, right_gate[1])
    u_ref[0] = h0[:width] - h1[width:]
    u_ref[1] = h0[width:] + h1[:width]
    mix = jnp.concatenate([mix_rows[0], mix_rows[1]], axis=0)

    def amplitudes(j, low, right, write):
        at = pl.ds(pl.multiple_of(j * low_width, low_width), low_width)
        u = jnp.concatenate([u_ref[0, at, :], u_ref[1, at, :]], axis=0).astype(jnp.bfloat16)
        index_rows, lanes = low.shape
        part = 2 if index_rows % 2 == 0 else 1
        for k in range(0, index_rows, part):
            x = dot(mix, onehot(low[k : k + part], width))
            v = dot(u, onehot(right[k : k + part], width))
            x0, x1, v0, v1 = x[:low_width], x[low_width:], v[:low_width], v[low_width:]
            real = jnp.sum(x0 * v0 - x1 * v1, axis=0, keepdims=True)
            imag = jnp.sum(x0 * v1 + x1 * v0, axis=0, keepdims=True)
            write(pl.ds(k * lanes, part * lanes), jnp.concatenate([real, imag], axis=0))

    def write_own(at, value):
        own_ref[:, at] = value

    amplitudes(me, idx_buf[0, 0], idx_buf[0, 1], write_own)

    z_copies = []
    for n, (x, peer) in enumerate(z_peers):
        idx_copies[2 * n].wait_recv()
        idx_copies[2 * n + 1].wait_recv()

        def write_send(at, value, x=x):
            z_send[x, :, at] = value.astype(z_send.dtype)

        amplitudes(peer["bits"], idx_buf[x, 0], idx_buf[x, 1], write_send)
        copy = pltpu.make_async_remote_copy(
            src_ref=z_send.at[x], dst_ref=z_recv.at[x],
            send_sem=z_send_sem.at[x], recv_sem=z_recv_sem.at[x],
            device_id=peer, device_id_type=MESH,
        )
        copy.start()
        z_copies.append(copy)

    own = own_ref[...]
    for x in range(1, groups):
        z_copies[x - 1].wait_recv()
        own = own + z_recv[x].astype(jnp.float32)
    here = sec * reps + rep
    plane[here] = own.astype(plane.dtype)
    p_copies = []
    for there, peer, n in plane_peers:
        copy = pltpu.make_async_remote_copy(
            src_ref=plane.at[here], dst_ref=plane.at[here],
            send_sem=p_send_sem.at[n], recv_sem=p_recv_sem.at[n],
            device_id=peer, device_id_type=MESH,
        )
        copy.start()
        p_copies.append(copy)
    for copy in p_copies:
        copy.wait_recv()
    result = plane[0].astype(jnp.float32)
    for n in range(1, sections * reps):
        result = result + plane[n].astype(jnp.float32)
    out_ref[...] = result * norm
    for copy in idx_copies + z_copies + p_copies:
        copy.wait_send()


def body(left_stems, right_stems, left_gate, mix_gate, right_gate, left_low, right_index):
    width = left_gate.shape[1]
    sizes = tuple(lax.axis_size(name) for name in ("bits", "section", "rep"))
    groups, sections, reps = sizes
    pairs = left_stems.shape[0] * left_stems.shape[1]
    norm = 1.0 / math.sqrt(pairs * sections * reps)
    count = left_low.shape[0]
    index_shape = (count // 128, 128)
    bf16, f32 = jnp.bfloat16, jnp.float32
    hbm = pl.BlockSpec(memory_space=pltpu.HBM)
    vmem = pl.BlockSpec(memory_space=pltpu.VMEM)
    dma = pltpu.SemaphoreType.DMA
    keep = functools.partial(pltpu.with_memory_space_constraint, memory_space=pltpu.HBM)
    return pl.pallas_call(
        functools.partial(kernel, sizes, norm),
        out_shape=jax.ShapeDtypeStruct((2, count), f32),
        in_specs=[hbm] * 7,
        out_specs=vmem,
        scratch_shapes=[
            pltpu.VMEM((2 * pairs, width), bf16),
            pltpu.VMEM((2 * pairs, width), bf16),
            pltpu.VMEM((2, width, width), bf16),
            pltpu.VMEM((2, width // groups, width), bf16),
            pltpu.VMEM((2, width, width), bf16),
            pltpu.VMEM((2, width, width), f32),
            pltpu.VMEM((groups, 2) + index_shape, jnp.int32),
            pltpu.VMEM((2, count), f32),
            pltpu.VMEM((groups, 2, count), bf16),
            pltpu.VMEM((groups, 2, count), bf16),
            pltpu.VMEM((sections * reps, 2, count), bf16),
            dma((2, CHUNKS)),
            dma((3,)),
            dma((groups, 2)),
            dma((groups, 2)),
            dma((groups,)),
            dma((groups,)),
            dma((sections * reps,)),
            dma((sections * reps,)),
        ],
        compiler_params=pltpu.CompilerParams(
            collective_id=0, has_side_effects=True, vmem_limit_bytes=16 * 1024 * 1024
        ),
        name="amplitudes",
    )(
        keep(left_stems.reshape(pairs, 2, width)), keep(right_stems.reshape(pairs, 2, width)),
        keep(left_gate), keep(mix_gate), keep(right_gate),
        keep(left_low.reshape(index_shape)), keep(right_index.reshape(index_shape)),
    )


def solution(mesh):
    in_specs = (
        P("rep", "section", None, "bits", None),
        P("rep", "section", None, None),
        P(),
        P(),
        P(),
        P("bits"),
        P("bits"),
    )
    out_specs = P(None, "bits")
    return jax.shard_map(body, mesh=mesh, in_specs=in_specs, out_specs=out_specs, check_vma=False)
```
